256 devices in a mesh: dp: 16 (over x, y), expert: 16 (over z, core).
Axes of the slice: x: 4, y: 4, z: 8, core: 2. Of those that a mesh axis runs over, the one named last changes fastest.
Arguments:
- tokens: bfloat16 [32768, 2048], P(('dp', 'expert')), may hold values from -6 to 6
- cotangent: bfloat16 [32768, 2048], P(('dp', 'expert')), may hold values from -1.5 to 1.5
- expert_ids: int32 [32768, 8], P(('dp', 'expert')), may hold values from 0 to 127, as said below
- gate_values: float32 [32768, 8], P(('dp', 'expert')), may hold values from 0.1 to 0.5
- w_gate: bfloat16 [2048, 16, 768], P(None, 'expert'), may hold values from -0.125 to 0.125
- w_up: bfloat16 [2048, 16, 768], P(None, 'expert'), may hold values from -0.125 to 0.125
- w_down: bfloat16 [2048, 16, 768], P(None, 'expert'), may hold values from -0.21875 to 0.21875
Outputs:
- output: bfloat16 [32768, 2048], P(('dp', 'expert'))
- grad_input: bfloat16 [32768, 2048], P(('dp', 'expert'))
- grad_gate: float32 [2048, 16, 768], P('dp', 'expert')
- grad_up: float32 [2048, 16, 768], P('dp', 'expert')
- grad_down: float32 [2048, 16, 768], P('dp', 'expert')
The draws below stay inside these ranges and needn't reach their ends.
Inputs may be any that keep to these rules, and one draw needn't show every extreme that they name: `expert_ids`: each row names 8 different experts in any order. In the rows of one device no expert under 16 is named more than 32 times; in each group of 2048 rows (one index of dp) one expert under 16 is named exactly 32 times by the rows of every device of the group.
All inputs are finite; a program needn't handle non-finite values.
Results may differ from the reference program's by a relative error of at most 0.013.
Values may be sent and summed in bfloat16 or wider, within the bound.
No kernel may reach another device: no remote copies, remote signals or barrier semaphores. Data moves between devices by JAX's collectives and lax.ppermute only.
A program may use at most 128 MiB of HBM per device.

```python
import jax
import jax.numpy as jnp
from jax import lax

D = 2048
FW = 768
TOPK = 8
EXPERTS_ALL = 128
TOK_DEV = 128
CAP = 32
EXPERTS = 16
GROUP_TOK = 2048
TOKENS = 32768
N_EXPERT = 16


def draw_expert_ids(key, part):
    key_hot, key_pick, key_rot, key_second, key_outer, key_order = jax.random.split(key, 6)
    blocks = TOKENS // TOK_DEV
    groups = TOKENS // GROUP_TOK
    hot = jax.random.randint(key_hot, (groups,), 0, EXPERTS).astype(jnp.int32)
    block_group = jnp.arange(blocks, dtype=jnp.int32) // (GROUP_TOK // TOK_DEV)
    hot_block = hot[block_group][:, None]
    local_range = jnp.arange(TOK_DEV, dtype=jnp.int32)
    pick_score = jax.random.randint(key_pick, (blocks, TOK_DEV), 0, 1 << 20) * TOK_DEV + local_range[None, :]
    position = jnp.argsort(jnp.argsort(pick_score, axis=1, stable=True), axis=1, stable=True).astype(jnp.int32)
    takes_hot = position < CAP
    rotation = jax.random.randint(key_rot, (blocks, 1), 0, EXPERTS - 1).astype(jnp.int32)
    other_index = (position + rotation) % (EXPERTS - 1)
    other_expert = other_index + (other_index >= hot_block).astype(jnp.int32)
    has_second = jax.random.randint(key_second, (blocks, TOK_DEV), 0, 4) > 0
    outside_count = EXPERTS_ALL - EXPERTS
    outer_score = jax.random.randint(key_outer, (TOKENS, outside_count), 0, 1 << 20) * outside_count + jnp.arange(outside_count, dtype=jnp.int32)[None, :]
    outer_values, outer_picked = lax.top_k(outer_score, TOPK)
    outer_ids = outer_picked.astype(jnp.int32).reshape(blocks, TOK_DEV, TOPK) + EXPERTS
    first = jnp.where(takes_hot, hot_block, outer_ids[:, :, 0])
    second = jnp.where(has_second, other_expert, outer_ids[:, :, 1])
    columns = jnp.concatenate((first[:, :, None], second[:, :, None], outer_ids[:, :, 2:]), axis=2)
    columns = columns.reshape(TOKENS, TOPK)
    order_score = jax.random.randint(key_order, (TOKENS, TOPK), 0, 1 << 20) * TOPK + jnp.arange(TOPK, dtype=jnp.int32)[None, :]
    order = jnp.argsort(order_score, axis=1, stable=True)
    return jnp.take_along_axis(columns, order, axis=1).astype(jnp.int32)


def steps_of(key, dims, cuts, smallest, largest):
    factor_of = 1.0
    for axis_at, blocks in cuts:
        draws = jax.random.uniform(jax.random.fold_in(jax.random.fold_in(key, 6), axis_at), (blocks,), jnp.float32, smallest / len(cuts), largest / len(cuts))
        factor_of = factor_of * jnp.repeat(jnp.exp(draws), dims[axis_at] // blocks).reshape((-1,) + (1,) * (len(dims) - 1 - axis_at))
    return factor_of


def bell_draw(stream_key, extent, deviation, reach, cuts=(), held_as=jnp.bfloat16):
    drawn = deviation * jax.random.normal(stream_key, extent, jnp.float32)
    if cuts:
        drawn = drawn * steps_of(stream_key, extent, cuts, -0.22, 0.18)
    return jnp.clip(drawn, -reach, reach).astype(held_as)


def setup_inputs(seed: int = 0) -> dict:
    key_of = jax.random.split(jax.random.key(seed), 8)
    return {
        "tokens": bell_draw(key_of[0], (TOKENS, D), 1.0, 6.0, ((0, 256),)),
        "cotangent": bell_draw(key_of[1], (TOKENS, D), 0.25, 1.5, ((0, 256),)),
        "expert_ids": draw_expert_ids(jax.random.fold_in(key_of[7], 71), 0),
        "gate_values": jnp.clip(0.1 + 0.4 * jax.random.uniform(key_of[3], (TOKENS, TOPK), jnp.float32) ** steps_of(key_of[3], (TOKENS, TOPK), ((0, 256),), -0.2, 0.2), 0.1, 0.5),
        "w_gate": bell_draw(key_of[4], (D, EXPERTS, FW), D ** -0.5, 0.125, ((1, 16),)),
        "w_up": bell_draw(key_of[5], (D, EXPERTS, FW), D ** -0.5, 0.125, ((1, 16),)),
        "w_down": bell_draw(key_of[6], (D, EXPERTS, FW), FW ** -0.5, 0.21875, ((1, 16),)),
    }


def reference(tokens, cotangent, expert_ids, gate_values, w_gate, w_up, w_down):
    blocks = tokens.shape[0] // TOK_DEV
    groups = blocks // N_EXPERT
    experts_all = w_gate.shape[1]
    x_blocks = tokens.reshape(blocks, TOK_DEV, D).astype(jnp.float32)
    dy_blocks = cotangent.reshape(blocks, TOK_DEV, D).astype(jnp.float32)
    ids = expert_ids.reshape(blocks, TOK_DEV, TOPK)
    gates = gate_values.reshape(blocks, TOK_DEV, TOPK)
    expert_range = jnp.arange(experts_all, dtype=jnp.int32)
    chosen = (ids[..., None] == expert_range).astype(jnp.int32)
    present = jnp.sum(chosen, axis=2, dtype=jnp.int32)
    earlier = jnp.cumsum(present, axis=1, dtype=jnp.int32) - present
    weight_of = jnp.sum(chosen.astype(jnp.float32) * gates[..., None], axis=2)
    slot_range = jnp.arange(CAP, dtype=jnp.int32)
    highest = lax.Precision.HIGHEST

    def group_sum(left, right):
        left_g = left.reshape(groups, -1, left.shape[-1]).astype(jnp.float32)
        right_g = right.reshape(groups, -1, right.shape[-1]).astype(jnp.float32)
        partial_value = jnp.einsum("grd,grf->gdf", left_g, right_g, precision=highest).astype(jnp.bfloat16)
        partial_value = lax.optimization_barrier(partial_value)
        return jnp.sum(partial_value.astype(jnp.float32), axis=0)

    def one_expert(carry, expert):
        total_out, total_dx = carry
        here = lax.dynamic_index_in_dim(present, expert, 2, keepdims=False)
        rank_here = lax.dynamic_index_in_dim(earlier, expert, 2, keepdims=False)
        gate_here = lax.dynamic_index_in_dim(weight_of, expert, 2, keepdims=False)
        place = ((rank_here[:, :, None] == slot_range[None, None, :]) & (here[:, :, None] > 0)).astype(jnp.float32)
        weighted = place * gate_here[:, :, None]
        x_slots = jnp.einsum("btc,btd->bcd", place, x_blocks, precision=highest).astype(jnp.bfloat16)
        z_slots = jnp.einsum("btc,btd->bcd", weighted, dy_blocks, precision=highest).astype(jnp.bfloat16)
        x_rows = x_slots.reshape(-1, D)
        z_rows = z_slots.reshape(-1, D)
        wg = lax.dynamic_index_in_dim(w_gate, expert, 1, keepdims=False)
        wu = lax.dynamic_index_in_dim(w_up, expert, 1, keepdims=False)
        wd = lax.dynamic_index_in_dim(w_down, expert, 1, keepdims=False)
        gate_pre = jnp.dot(x_rows, wg, preferred_element_type=jnp.float32)
        up_pre = jnp.dot(x_rows, wu, preferred_element_type=jnp.float32)
        sig = jax.nn.sigmoid(gate_pre)
        hidden = (gate_pre * sig * up_pre).astype(jnp.bfloat16)
        slot_out = jnp.dot(hidden, wd.T, preferred_element_type=jnp.float32).astype(jnp.bfloat16)
        d_hidden = jnp.dot(z_rows, wd, preferred_element_type=jnp.float32)
        d_gate = (d_hidden * up_pre * sig * (1.0 + gate_pre * (1.0 - sig))).astype(jnp.bfloat16)
        d_up = (d_hidden * gate_pre * sig).astype(jnp.bfloat16)
        slot_dx = (jnp.dot(d_gate, wg.T, preferred_element_type=jnp.float32)
                   + jnp.dot(d_up, wu.T, preferred_element_type=jnp.float32)).astype(jnp.bfloat16)
        grad_g = group_sum(x_rows, d_gate)
        grad_u = group_sum(x_rows, d_up)
        grad_d = group_sum(z_rows, hidden)
        out_blocks = slot_out.reshape(blocks, CAP, D).astype(jnp.float32)
        dx_blocks = slot_dx.reshape(blocks, CAP, D).astype(jnp.float32)
        total_out = total_out + jnp.einsum("btc,bcd->btd", weighted, out_blocks, precision=highest)
        total_dx = total_dx + jnp.einsum("btc,bcd->btd", place, dx_blocks, precision=highest)
        return (total_out, total_dx), (grad_g, grad_u, grad_d)

    start = (jnp.zeros((blocks, TOK_DEV, D), jnp.float32), jnp.zeros((blocks, TOK_DEV, D), jnp.float32))
    (total_out, total_dx), (grad_g, grad_u, grad_d) = lax.scan(one_expert, start, expert_range)
    output = total_out.reshape(-1, D).astype(jnp.bfloat16)
    grad_input = total_dx.reshape(-1, D).astype(jnp.bfloat16)
    return (output, grad_input, jnp.transpose(grad_g, (1, 0, 2)), jnp.transpose(grad_u, (1, 0, 2)),
            jnp.transpose(grad_d, (1, 0, 2)))
```

```python
import functools

import jax
import jax.numpy as jnp
from jax import lax
from jax.experimental import pallas as pl
from jax.experimental.pallas import tpu as pltpu
from jax.sharding import PartitionSpec as P


BF = jnp.bfloat16
F32 = jnp.float32
ANY = pl.BlockSpec(memory_space=pltpu.HBM)
VM = pl.BlockSpec(memory_space=pltpu.VMEM)
SM = pl.BlockSpec(memory_space=pltpu.SMEM)
PARAMS = pltpu.CompilerParams(vmem_limit_bytes=56 * 1024 * 1024)


def shape_of(shape, dtype):
    return jax.ShapeDtypeStruct(shape, dtype)


def moves_of(owners):
    chips = owners // 2
    far = sorted(range(1, chips), key=lambda d: -min(d, chips - d))
    return [(0, 0)] + [(d, c) for d in far for c in (0, 1)] + [(0, 1)]


def pairs_of(owners, move, sign):
    chips = owners // 2
    return [
        (z * 2 + c, ((z + sign * move[0]) % chips) * 2 + (c ^ move[1]))
        for z in range(chips)
        for c in range(2)
    ]


def target(me, move, chips):
    return lax.rem(me // 2 + move[0], chips) * 2 + lax.rem(lax.rem(me, 2) + move[1], 2)


def slots_kernel(moves, cap, me_ref, ids_ref, gates_ref, tok_ref, *refs):
    owners = len(moves)
    outs = refs[:owners]
    sel_ref, wt_ref = refs[owners : owners + 2]
    rank_s, gate_s = refs[owners + 2 :]
    topk, toks = ids_ref.shape
    expert = lax.broadcasted_iota(jnp.int32, (owners, toks), 0)
    present = jnp.zeros((owners, toks), F32)
    gate = jnp.zeros((owners, toks), F32)
    for k in range(topk):
        hit = ids_ref[k : k + 1, :] == expert
        present = present + jnp.where(hit, 1.0, 0.0)
        gate = gate + jnp.where(hit, gates_ref[k : k + 1, :], 0.0)
    before = lax.broadcasted_iota(jnp.int32, (toks, toks), 0) < lax.broadcasted_iota(
        jnp.int32, (toks, toks), 1
    )
    earlier = jnp.dot(
        present.astype(BF), jnp.where(before, 1.0, 0.0).astype(BF), preferred_element_type=F32
    )
    rank_s[...] = jnp.where(present > 0.0, earlier, -1.0).astype(jnp.int32)
    gate_s[...] = gate
    slot = lax.broadcasted_iota(jnp.int32, (cap, toks), 0)
    for j, move in enumerate(moves):
        e = target(me_ref[0], move, owners // 2)
        hit = rank_s[pl.ds(e, 1), :] == slot
        sel_ref[j * cap : (j + 1) * cap, :] = jnp.where(hit, 1.0, 0.0).astype(BF)
        wt_ref[j * cap : (j + 1) * cap, :] = jnp.where(hit, gate_s[pl.ds(e, 1), :], 0.0)
    rows = jnp.dot(sel_ref[...], tok_ref[...], preferred_element_type=F32).astype(BF)
    for j in range(owners):
        outs[j][...] = rows[j * cap : (j + 1) * cap, :]


def make_slots(me, ids, gates, tokens, moves, cap):
    owners = len(moves)
    toks, width = tokens.shape
    return pl.pallas_call(
        functools.partial(slots_kernel, moves, cap),
        out_shape=[shape_of((cap, width), BF)] * owners
        + [shape_of((owners * cap, toks), BF), shape_of((owners * cap, toks), F32)],
        in_specs=[SM, VM, VM, VM],
        out_specs=[VM] * (owners + 2),
        scratch_shapes=[pltpu.VMEM((owners, toks), jnp.int32), pltpu.VMEM((owners, toks), F32)],
        compiler_params=PARAMS,
        name="slots",
    )(me, ids, gates, tokens)


def gated_kernel(owners, cap, sel_ref, wt_ref, cot_ref, *outs):
    rows = jnp.dot(sel_ref[...], cot_ref[...], preferred_element_type=F32)
    gate = jnp.sum(wt_ref[...], axis=1, keepdims=True)
    rows = (rows * gate).astype(BF)
    for j in range(owners):
        outs[j][...] = rows[j * cap : (j + 1) * cap, :]


def make_gated(sel, wt, cot, owners, cap):
    return pl.pallas_call(
        functools.partial(gated_kernel, owners, cap),
        out_shape=[shape_of((cap, cot.shape[1]), BF)] * owners,
        in_specs=[VM] * 3,
        out_specs=[VM] * owners,
        compiler_params=PARAMS,
        name="gated",
    )(sel, wt, cot)


def gather_rows(pieces, rows, sems):
    cap = pieces[0].shape[0]
    copies = [
        pltpu.make_async_copy(p, rows.at[pl.ds(j * cap, cap), :], sems.at[j])
        for j, p in enumerate(pieces)
    ]
    for c in copies:
        c.start()
    return copies


def forward_kernel(owners, *refs):
    pieces = refs[:owners]
    wg, wu, wd = refs[owners : owners + 3]
    rows, gp, up, hid = refs[owners + 3 : owners + 7]
    outs = refs[owners + 7 : 2 * owners + 7]
    wg_s, wu_s, wd_s, sems = refs[2 * owners + 7 :]
    copies = gather_rows(pieces, rows, sems)
    weights = [
        pltpu.make_async_copy(a, b, sems.at[owners + i])
        for i, (a, b) in enumerate(((wg, wg_s), (wu, wu_s), (wd, wd_s)))
    ]
    for c in weights:
        c.start()
    for c in copies + weights[:2]:
        c.wait()
    cap = pieces[0].shape[0]
    step = min(256, owners * cap)

    @pl.loop(0, owners * cap // step)
    def _(i):
        part = pl.ds(pl.multiple_of(i * step, step), step)
        g = jnp.dot(rows[part, :], wg_s[...], preferred_element_type=F32)
        u = jnp.dot(rows[part, :], wu_s[...], preferred_element_type=F32)
        gp[part, :] = g
        up[part, :] = u
        hid[part, :] = (g * jax.nn.sigmoid(g) * u).astype(BF)

    weights[2].wait()
    for m in range(0, owners * cap, step):
        out = lax.dot_general(
            hid[m : m + step, :], wd_s[...], (((1,), (1,)), ((), ())), preferred_element_type=F32
        ).astype(BF)
        for i in range(step // cap):
            outs[m // cap + i][...] = out[i * cap : (i + 1) * cap, :]


def forward(pieces, wg, wu, wd):
    owners = len(pieces)
    cap, width = pieces[0].shape
    slots, fw = owners * cap, wg.shape[1]
    return pl.pallas_call(
        functools.partial(forward_kernel, owners),
        out_shape=[
            shape_of((slots, width), BF),
            shape_of((slots, fw), F32),
            shape_of((slots, fw), F32),
            shape_of((slots, fw), BF),
        ]
        + [shape_of((cap, width), BF)] * owners,
        in_specs=[ANY] * (owners + 3),
        out_specs=[VM] * (owners + 4),
        scratch_shapes=[pltpu.VMEM((width, fw), BF)] * 3 + [pltpu.SemaphoreType.DMA((owners + 3,))],
        compiler_params=PARAMS,
        name="forward",
    )(*pieces, wg, wu, wd)


def factors_kernel(gp, up, fg, fu):
    g = gp[...]
    s = jax.nn.sigmoid(g)
    fg[...] = up[...] * s * (1.0 + g * (1.0 - s))
    fu[...] = g * s


def factors(gp, up):
    slots, fw = gp.shape
    step = min(128, slots)
    some = pl.BlockSpec((step, fw), lambda i: (i, 0))
    return pl.pallas_call(
        factors_kernel,
        out_shape=[shape_of((slots, fw), F32)] * 2,
        grid=(slots // step,),
        in_specs=[some] * 2,
        out_specs=[some] * 2,
        compiler_params=PARAMS,
        name="factors",
    )(gp, up)


def backward_kernel(owners, *refs):
    pieces = refs[:owners]
    wd, fg, fu = refs[owners : owners + 3]
    rows, dg, du = refs[owners + 3 : owners + 6]
    wd_s, sems = refs[owners + 6 :]
    copies = gather_rows(pieces, rows, sems)
    weight = pltpu.make_async_copy(wd, wd_s, sems.at[owners])
    weight.start()
    for c in copies + [weight]:
        c.wait()
    slots = rows.shape[0]
    step = min(256, slots)

    @pl.loop(0, slots // step)
    def _(i):
        part = pl.ds(pl.multiple_of(i * step, step), step)
        dh = jnp.dot(rows[part, :], wd_s[...], preferred_element_type=F32)
        dg[part, :] = (dh * fg[part, :]).astype(BF)
        du[part, :] = (dh * fu[part, :]).astype(BF)


def backward(pieces, wd, fg, fu):
    owners = len(pieces)
    _, width = pieces[0].shape
    slots, fw = fg.shape
    return pl.pallas_call(
        functools.partial(backward_kernel, owners),
        out_shape=[shape_of((slots, width), BF), shape_of((slots, fw), BF), shape_of((slots, fw), BF)],
        in_specs=[ANY] * (owners + 1) + [VM] * 2,
        out_specs=[VM] * 3,
        scratch_shapes=[pltpu.VMEM((width, fw), BF), pltpu.SemaphoreType.DMA((owners + 1,))],
        compiler_params=PARAMS,
        name="backward",
    )(*pieces, wd, fg, fu)


def wgrad_kernel(nx, ny, xy_ref, x_ref, z_ref, dg_ref, du_ref, hid_ref, *refs):
    a_refs, b_refs = refs[:nx], refs[nx : nx + ny]
    acc, sems = refs[nx + ny :]
    jx = pl.program_id(0)
    fw = dg_ref.shape[1]
    half = 3 * fw // 2
    block = acc.shape[1] // ny
    dims = (((0,), (0,)), ((), ()))
    xb = x_ref[...]
    acc[jx, :, 0:fw] = lax.dot_general(xb, dg_ref[...], dims, preferred_element_type=F32).astype(BF)
    acc[jx, :, fw : 2 * fw] = lax.dot_general(
        xb, du_ref[...], dims, preferred_element_type=F32
    ).astype(BF)
    acc[jx, :, 2 * fw : 3 * fw] = lax.dot_general(
        z_ref[...], hid_ref[...], dims, preferred_element_type=F32
    ).astype(BF)

    def copies(j):
        out = []
        for k in range(ny):
            at = pl.ds(pl.multiple_of(lax.rem(xy_ref[1] + k, ny) * block, block), block)
            out.append((acc.at[j, at, pl.ds(0, half)], a_refs[j].at[k], sems.at[j, k, 0]))
            out.append((acc.at[j, at, pl.ds(half, half)], b_refs[k].at[j], sems.at[j, k, 1]))
        return out

    for j in range(nx):

        @pl.when(jx == j)
        def _(j=j):
            for c in copies(j):
                pltpu.make_async_copy(*c).start()

    @pl.when(jx == nx - 1)
    def _():
        for j in range(nx):
            for c in copies(j):
                pltpu.make_async_copy(*c).wait()


def wgrads(xy, rows, zrows, dg, du, hid, nx, ny):
    slots, width = rows.shape
    fw = dg.shape[1]
    wide = width // nx
    block = wide // ny
    half = 3 * fw // 2
    whole = pl.BlockSpec((slots, fw), lambda i, xy: (0, 0))
    cols = pl.BlockSpec((slots, wide), lambda i, xy: (0, lax.rem(xy[0] + i, nx)))
    return pl.pallas_call(
        functools.partial(wgrad_kernel, nx, ny),
        out_shape=[shape_of((ny, block, half), BF)] * nx + [shape_of((nx, block, half), BF)] * ny,
        grid_spec=pltpu.PrefetchScalarGridSpec(
            num_scalar_prefetch=1,
            grid=(nx,),
            in_specs=[cols, cols, whole, whole, whole],
            out_specs=[ANY] * (nx + ny),
            scratch_shapes=[
                pltpu.VMEM((nx, wide, 3 * fw), BF),
                pltpu.SemaphoreType.DMA((nx, ny, 2)),
            ],
        ),
        compiler_params=pltpu.CompilerParams(
            dimension_semantics=("arbitrary",), vmem_limit_bytes=56 * 1024 * 1024
        ),
        name="wgrads",
    )(xy, rows, zrows, dg, du, hid)


def slot_dx_kernel(owners, dg_ref, du_ref, wg_ref, wu_ref, *outs):
    dims = (((1,), (1,)), ((), ()))
    cap = outs[0].shape[0]
    out = lax.dot_general(dg_ref[...], wg_ref[...], dims, preferred_element_type=F32)
    out = out + lax.dot_general(du_ref[...], wu_ref[...], dims, preferred_element_type=F32)
    out = out.astype(BF)
    for j in range(owners):
        outs[j][...] = out[j * cap : (j + 1) * cap, :]


def slot_dx(dg, du, wg, wu, owners):
    slots, fw = dg.shape
    width = wg.shape[0]
    cap = slots // owners
    wide = min(512, width)
    whole = pl.BlockSpec((slots, fw), lambda i: (0, 0))
    some = pl.BlockSpec((wide, fw), lambda i: (i, 0))
    return pl.pallas_call(
        functools.partial(slot_dx_kernel, owners),
        out_shape=[shape_of((cap, width), BF)] * owners,
        grid=(width // wide,),
        in_specs=[whole, whole, some, some],
        out_specs=[pl.BlockSpec((cap, wide), lambda i: (0, i))] * owners,
        compiler_params=PARAMS,
        name="slot_dx",
    )(dg, du, wg, wu)


def combine_kernel(owners, terms, mat_ref, *refs):
    pieces, out, rows, sems = refs[:owners], refs[owners], refs[owners + 1], refs[owners + 2]
    copies = gather_rows(pieces, rows, sems)
    dims = (((0,), (0,)), ((), ()))
    left = mat_ref[...]
    parts = []
    for _ in range(terms):
        high = left.astype(BF)
        parts.append(high)
        left = left - high.astype(left.dtype)
    for c in copies:
        c.wait()
    total = lax.dot_general(parts[0], rows[...], dims, preferred_element_type=F32)
    for part in parts[1:]:
        total = total + lax.dot_general(part, rows[...], dims, preferred_element_type=F32)
    out[...] = total.astype(BF)


def combine(mat, pieces, terms):
    owners = len(pieces)
    cap, width = pieces[0].shape
    return pl.pallas_call(
        functools.partial(combine_kernel, owners, terms),
        out_shape=shape_of((mat.shape[1], width), BF),
        in_specs=[VM] + [ANY] * owners,
        out_specs=VM,
        scratch_shapes=[
            pltpu.VMEM((owners * cap, width), BF),
            pltpu.SemaphoreType.DMA((owners,)),
        ],
        compiler_params=PARAMS,
    )(mat, *pieces)


def fold_kernel(nx, ny, *refs):
    a, b = refs[:nx], refs[nx : nx + ny]
    outs = refs[nx + ny :]
    for k in range(ny):
        total = a[0][k].astype(F32)
        for r in a[1:]:
            total = total + r[k].astype(F32)
        outs[k][...] = total.astype(outs[k].dtype)
    for k in range(nx):
        total = b[0][k].astype(F32)
        for r in b[1:]:
            total = total + r[k].astype(F32)
        outs[ny + k][...] = total.astype(outs[ny + k].dtype)


def fold(a, b):
    nx, ny = len(a), len(b)
    _, block, half = a[0].shape
    mine, theirs = shape_of((block, half), F32), shape_of((block, half), BF)
    out = pl.pallas_call(
        functools.partial(fold_kernel, nx, ny),
        out_shape=[mine] + [theirs] * (ny - 1) + [mine] + [theirs] * (nx - 1),
        in_specs=[VM] * (nx + ny),
        out_specs=[VM] * (nx + ny),
        compiler_params=PARAMS,
        name="fold",
    )(*a, *b)
    return out[:ny], out[ny:]


def last_kernel(na, nb, *refs):
    a, b = refs[:na], refs[na : na + nb]
    gate, up, down = refs[na + nb :]
    left, right = a[0][...], b[0][...]
    for r in a[1:]:
        left = left + r[...].astype(F32)
    for r in b[1:]:
        right = right + r[...].astype(F32)
    fw = gate.shape[2]
    cut = left.shape[1] - fw
    gate[:, 0, :] = left[:, :fw]
    up[:, 0, :cut] = left[:, fw:]
    up[:, 0, cut:] = right[:, : fw - cut]
    down[:, 0, :] = right[:, fw - cut :]


def last(a, b):
    block, half = a[0].shape
    fw = 2 * half // 3
    return pl.pallas_call(
        functools.partial(last_kernel, len(a), len(b)),
        out_shape=[shape_of((block, 1, fw), F32)] * 3,
        in_specs=[VM] * (len(a) + len(b)),
        out_specs=[VM] * 3,
        compiler_params=PARAMS,
        name="last",
    )(*a, *b)


def per_device(tokens, cotangent, expert_ids, gate_values, w_gate, w_up, w_down):
    owners = lax.axis_size("expert")
    groups = lax.axis_size("dp")
    nx = int(round(groups**0.5))
    ny = groups // nx
    cap = tokens.shape[0] // 4
    width, _, fw = w_gate.shape
    wg, wu, wd = (w.reshape(width, fw) for w in (w_gate, w_up, w_down))
    moves = moves_of(owners)
    me = lax.axis_index("expert").astype(jnp.int32)[None]
    group = lax.axis_index("dp").astype(jnp.int32)
    xy = jnp.stack([group // ny, lax.rem(group, ny)])

    def send(pieces, sign):
        return [pieces[0]] + [
            lax.ppermute(p, "expert", pairs_of(owners, m, sign))
            for p, m in zip(pieces[1:], moves[1:])
        ]

    def shift(piece, dx, dy):
        pairs = [
            (x * ny + y, ((x + dx) % nx) * ny + (y + dy) % ny) for x in range(nx) for y in range(ny)
        ]
        return lax.ppermute(piece, "dp", pairs)

    def far_first(n):
        return sorted(range(1, n), key=lambda d: -min(d, n - d))

    *x_out, sel, wt = make_slots(me, expert_ids.T, gate_values.T, tokens, moves, cap)
    x_in = send(x_out, 1)
    z_out = make_gated(sel, wt, cotangent, owners, cap)
    z_in = send(z_out, 1)
    rows, gp, up, hid, *s_out = forward(x_in, wg, wu, wd)
    s_in = send(s_out, -1)
    fg, fu = factors(gp, up)
    zrows, dg, du = backward(z_in, wd, fg, fu)
    parts = wgrads(xy, rows, zrows, dg, du, hid, nx, ny)
    a, b = parts[:nx], parts[nx:]
    a_in, b_in = [a[0]], [b[0]]
    for d in far_first(nx):
        a_in.append(shift(a[d], d, 0))
    for d in far_first(ny):
        b_in.append(shift(b[d], 0, d))
    d_out = slot_dx(dg, du, wg, wu, owners)
    d_in = send(d_out, -1)
    output = combine(wt, s_in, 3)
    a2, b2 = fold(a_in, b_in)
    a3, b3 = [a2[0]], [b2[0]]
    for d in far_first(ny):
        a3.append(shift(a2[d], 0, d))
    for d in far_first(nx):
        b3.append(shift(b2[d], d, 0))
    grad_input = combine(sel, d_in, 1)
    grads = last(a3, b3)
    return (output, grad_input, *grads)


def solution(mesh):
    return jax.shard_map(
        per_device,
        mesh=mesh,
        in_specs=(
            P(("dp", "expert"), None),
            P(("dp", "expert"), None),
            P(("dp", "expert"), None),
            P(("dp", "expert"), None),
            P(None, "expert", None),
            P(None, "expert", None),
            P(None, "expert", None),
        ),
        out_specs=(
            P(("dp", "expert"), None),
            P(("dp", "expert"), None),
            P("dp", "expert", None),
            P("dp", "expert", None),
            P("dp", "expert", None),
        ),
        check_vma=False,
    )
```

```python
import functools

import jax
import jax.numpy as jnp
from jax import lax
from jax.experimental import pallas as pl
from jax.experimental.pallas import tpu as pltpu
from jax.sharding import PartitionSpec as P


BF = jnp.bfloat16
F32 = jnp.float32
ANY = pl.BlockSpec(memory_space=pl.ANY)
VM = pl.BlockSpec(memory_space=pltpu.VMEM)
SM = pl.BlockSpec(memory_space=pltpu.SMEM)
PARAMS = pltpu.CompilerParams(vmem_limit_bytes=24 * 1024 * 1024)


def shape_of(shape, dtype):
    return jax.ShapeDtypeStruct(shape, dtype)


def far_first(n):
    return sorted(range(1, n), key=lambda d: -min(d, n - d))


def pairs_of(owners, chip, core):
    chips = owners // 2
    return [
        (z * 2 + c, ((z + chip) % chips) * 2 + (c ^ core)) for z in range(chips) for c in range(2)
    ]


def target(me, chip, chips):
    return lax.rem(me // 2 + chip, chips) * 2 + lax.rem(me, 2)


def slots_kernel(moves, owners, cap, me_ref, ids0, ids1, tok0, tok1, *refs):
    outs = refs[: len(moves)]
    sel_ref, rank_s = refs[len(moves) :]
    topk, toks = ids0.shape
    expert = lax.broadcasted_iota(jnp.int32, (owners, toks), 0)
    slot = lax.broadcasted_iota(jnp.int32, (cap, toks), 0)
    before = lax.broadcasted_iota(jnp.int32, (toks, toks), 0) < lax.broadcasted_iota(
        jnp.int32, (toks, toks), 1
    )
    before = jnp.where(before, 1.0, 0.0).astype(BF)
    for p, ids in enumerate((ids0, ids1)):
        present = jnp.zeros((owners, toks), F32)
        for k in range(topk):
            present = present + jnp.where(ids[k : k + 1, :] == expert, 1.0, 0.0)
        earlier = jnp.dot(present.astype(BF), before, preferred_element_type=F32)
        rank_s[p] = jnp.where(present > 0.0, earlier, -1.0).astype(jnp.int32)
    for p, tok in enumerate((tok0, tok1)):
        for j, move in enumerate(moves):
            e = target(me_ref[0], move, owners // 2)
            hit = rank_s[p, pl.ds(e, 1), :] == slot
            sel_ref[p, j * cap : (j + 1) * cap, :] = jnp.where(hit, 1.0, 0.0).astype(BF)
        rows = jnp.dot(sel_ref[p], tok[...], preferred_element_type=F32).astype(BF)
        for j in range(len(moves)):
            outs[j][p * cap : (p + 1) * cap, :] = rows[j * cap : (j + 1) * cap, :]


def make_slots(me, ids, tokens, moves, owners, cap):
    toks, width = tokens[0].shape
    n = len(moves)
    return pl.pallas_call(
        functools.partial(slots_kernel, moves, owners, cap),
        out_shape=[shape_of((2 * cap, width), BF)] * n + [shape_of((2, n * cap, toks), BF)],
        in_specs=[SM] + [VM] * 4,
        out_specs=[VM] * (n + 1),
        scratch_shapes=[pltpu.VMEM((2, owners, toks), jnp.int32)],
        compiler_params=PARAMS,
        name="slots",
    )(me, *ids, *tokens)


def gated_kernel(moves, owners, cap, me_ref, ids0, ids1, gates0, gates1, cot0, cot1, sel, *refs):
    outs = refs[: len(moves)]
    wt_ref, gate_s = refs[len(moves) :]
    topk, toks = ids0.shape
    expert = lax.broadcasted_iota(jnp.int32, (owners, toks), 0)
    for p, (ids, gates) in enumerate(((ids0, gates0), (ids1, gates1))):
        gate = jnp.zeros((owners, toks), F32)
        for k in range(topk):
            gate = gate + jnp.where(ids[k : k + 1, :] == expert, gates[k : k + 1, :], 0.0)
        gate_s[p] = gate
    for p, cot in enumerate((cot0, cot1)):
        for j, move in enumerate(moves):
            e = target(me_ref[0], move, owners // 2)
            part = pl.ds(j * cap, cap)
            wt_ref[p, part, :] = sel[p, part, :].astype(F32) * gate_s[p, pl.ds(e, 1), :]
        rows = jnp.dot(sel[p], cot[...], preferred_element_type=F32)
        rows = (rows * jnp.sum(wt_ref[p], axis=1, keepdims=True)).astype(BF)
        for j in range(len(moves)):
            outs[j][p * cap : (p + 1) * cap, :] = rows[j * cap : (j + 1) * cap, :]


def make_gated(me, ids, gates, cots, sel, moves, owners, cap):
    toks, width = cots[0].shape
    n = len(moves)
    return pl.pallas_call(
        functools.partial(gated_kernel, moves, owners, cap),
        out_shape=[shape_of((2 * cap, width), BF)] * n + [shape_of((2, n * cap, toks), F32)],
        in_specs=[SM] + [VM] * 7,
        out_specs=[VM] * (n + 1),
        scratch_shapes=[pltpu.VMEM((2, owners, toks), F32)],
        compiler_params=PARAMS,
        name="gated",
    )(me, *ids, *gates, *cots, sel)


def forward_kernel(n, *refs):
    pieces = refs[:n]
    wg, wu, wd = refs[n : n + 3]
    rows, gp, up, hid = refs[n + 3 : n + 7]
    outs = refs[n + 7 :]
    size = pieces[0].shape[0]
    for j, p in enumerate(pieces):
        rows[j * size : (j + 1) * size, :] = p[...]
    step = min(256, n * size)

    @pl.loop(0, n * size // step)
    def _(i):
        part = pl.ds(pl.multiple_of(i * step, step), step)
        g = jnp.dot(rows[part, :], wg[...], preferred_element_type=F32)
        u = jnp.dot(rows[part, :], wu[...], preferred_element_type=F32)
        gp[part, :] = g
        up[part, :] = u
        hid[part, :] = (g * jax.nn.sigmoid(g) * u).astype(BF)

    for m in range(0, n * size, step):
        out = lax.dot_general(
            hid[m : m + step, :], wd[...], (((1,), (1,)), ((), ())), preferred_element_type=F32
        ).astype(BF)
        for i in range(step // size):
            outs[m // size + i][...] = out[i * size : (i + 1) * size, :]


def forward(pieces, wg, wu, wd):
    n = len(pieces)
    size, width = pieces[0].shape
    slots, fw = n * size, wg.shape[1]
    return pl.pallas_call(
        functools.partial(forward_kernel, n),
        out_shape=[
            shape_of((slots, width), BF),
            shape_of((slots, fw), F32),
            shape_of((slots, fw), F32),
            shape_of((slots, fw), BF),
        ]
        + [shape_of((size, width), BF)] * n,
        in_specs=[VM] * (n + 3),
        out_specs=[VM] * (n + 4),
        compiler_params=PARAMS,
        name="forward",
    )(*pieces, wg, wu, wd)


def factors_kernel(gp, up, fg, fu):
    g = gp[...]
    s = jax.nn.sigmoid(g)
    fg[...] = up[...] * s * (1.0 + g * (1.0 - s))
    fu[...] = g * s


def factors(gp, up):
    slots, fw = gp.shape
    step = min(128, slots)
    some = pl.BlockSpec((step, fw), lambda i: (i, 0))
    return pl.pallas_call(
        factors_kernel,
        out_shape=[shape_of((slots, fw), F32)] * 2,
        grid=(slots // step,),
        in_specs=[some] * 2,
        out_specs=[some] * 2,
        compiler_params=PARAMS,
        name="factors",
    )(gp, up)


def backward_kernel(n, *refs):
    pieces = refs[:n]
    wd, fg, fu = refs[n : n + 3]
    rows, dg, du = refs[n + 3 :]
    size = pieces[0].shape[0]
    for j, p in enumerate(pieces):
        rows[j * size : (j + 1) * size, :] = p[...]
    slots = rows.shape[0]
    step = min(256, slots)

    @pl.loop(0, slots // step)
    def _(i):
        part = pl.ds(pl.multiple_of(i * step, step), step)
        dh = jnp.dot(rows[part, :], wd[...], preferred_element_type=F32)
        dg[part, :] = (dh * fg[part, :]).astype(BF)
        du[part, :] = (dh * fu[part, :]).astype(BF)


def backward(pieces, wd, fg, fu):
    n = len(pieces)
    slots, fw = fg.shape
    return pl.pallas_call(
        functools.partial(backward_kernel, n),
        out_shape=[shape_of((slots, wd.shape[0]), BF), shape_of((slots, fw), BF), shape_of((slots, fw), BF)],
        in_specs=[VM] * (n + 3),
        out_specs=[VM] * 3,
        compiler_params=PARAMS,
        name="backward",
    )(*pieces, wd, fg, fu)


def wgrad_kernel(nx, ny, xy_ref, x_ref, z_ref, dg_ref, du_ref, hid_ref, *refs):
    a_refs, b_refs = refs[:nx], refs[nx : nx + ny]
    acc, sems = refs[nx + ny :]
    jx = pl.program_id(0)
    fw = dg_ref.shape[1]
    half = 3 * fw // 2
    block = acc.shape[1] // ny
    dims = (((0,), (0,)), ((), ()))
    xb = x_ref[...]
    acc[jx, :, 0:fw] = lax.dot_general(xb, dg_ref[...], dims, preferred_element_type=F32).astype(BF)
    acc[jx, :, fw : 2 * fw] = lax.dot_general(
        xb, du_ref[...], dims, preferred_element_type=F32
    ).astype(BF)
    acc[jx, :, 2 * fw : 3 * fw] = lax.dot_general(
        z_ref[...], hid_ref[...], dims, preferred_element_type=F32
    ).astype(BF)

    def copies(j):
        out = []
        for k in range(ny):
            at = pl.ds(pl.multiple_of(lax.rem(xy_ref[1] + k, ny) * block, block), block)
            out.append((acc.at[j, at, pl.ds(0, half)], a_refs[j].at[k], sems.at[j, k, 0]))
            out.append((acc.at[j, at, pl.ds(half, half)], b_refs[k].at[j], sems.at[j, k, 1]))
        return out

    for j in range(nx):

        @pl.when(jx == j)
        def _(j=j):
            for c in copies(j):
                pltpu.make_async_copy(*c).start()

    @pl.when(jx == nx - 1)
    def _():
        for j in range(nx):
            for c in copies(j):
                pltpu.make_async_copy(*c).wait()


def wgrads(xy, rows, zrows, dg, du, hid, nx, ny):
    slots, width = rows.shape
    fw = dg.shape[1]
    wide = width // nx
    block = wide // ny
    half = 3 * fw // 2
    whole = pl.BlockSpec((slots, fw), lambda i, xy: (0, 0))
    cols = pl.BlockSpec((slots, wide), lambda i, xy: (0, lax.rem(xy[0] + i, nx)))
    return pl.pallas_call(
        functools.partial(wgrad_kernel, nx, ny),
        out_shape=[shape_of((ny, block, half), BF)] * nx + [shape_of((nx, block, half), BF)] * ny,
        grid_spec=pltpu.PrefetchScalarGridSpec(
            num_scalar_prefetch=1,
            grid=(nx,),
            in_specs=[cols, cols, whole, whole, whole],
            out_specs=[ANY] * (nx + ny),
            scratch_shapes=[
                pltpu.VMEM((nx, wide, 3 * fw), BF),
                pltpu.SemaphoreType.DMA((nx, ny, 2)),
            ],
        ),
        compiler_params=pltpu.CompilerParams(
            dimension_semantics=("arbitrary",), vmem_limit_bytes=24 * 1024 * 1024
        ),
        name="wgrads",
    )(xy, rows, zrows, dg, du, hid)


def slot_dx_kernel(owners, dg_ref, du_ref, wg_ref, wu_ref, *outs):
    dims = (((1,), (1,)), ((), ()))
    cap = outs[0].shape[0]
    out = lax.dot_general(dg_ref[...], wg_ref[...], dims, preferred_element_type=F32)
    out = out + lax.dot_general(du_ref[...], wu_ref[...], dims, preferred_element_type=F32)
    out = out.astype(BF)
    for j in range(owners):
        outs[j][...] = out[j * cap : (j + 1) * cap, :]


def slot_dx(dg, du, wg, wu, owners):
    slots, fw = dg.shape
    width = wg.shape[0]
    cap = slots // owners
    wide = min(512, width)
    whole = pl.BlockSpec((slots, fw), lambda i: (0, 0))
    some = pl.BlockSpec((wide, fw), lambda i: (i, 0))
    return pl.pallas_call(
        functools.partial(slot_dx_kernel, owners),
        out_shape=[shape_of((cap, width), BF)] * owners,
        grid=(width // wide,),
        in_specs=[whole, whole, some, some],
        out_specs=[pl.BlockSpec((cap, wide), lambda i: (0, i))] * owners,
        compiler_params=PARAMS,
        name="slot_dx",
    )(dg, du, wg, wu)


def combine_kernel(n, terms, mat_ref, *refs):
    pieces = refs[:n]
    outs, rows = refs[n : n + 2], refs[n + 2]
    size = pieces[0].shape[0]
    cap = size // 2
    dims = (((0,), (0,)), ((), ()))
    for p in (1, 0):
        for j, piece in enumerate(pieces):
            rows[j * cap : (j + 1) * cap, :] = piece[p * cap : (p + 1) * cap, :]
        left = mat_ref[p]
        total = None
        for _ in range(terms):
            high = left.astype(BF)
            left = left - high.astype(left.dtype)
            part = lax.dot_general(high, rows[...], dims, preferred_element_type=F32)
            total = part if total is None else total + part
        outs[p][...] = total


def combine(mat, pieces, terms):
    n = len(pieces)
    size, width = pieces[0].shape
    return pl.pallas_call(
        functools.partial(combine_kernel, n, terms),
        out_shape=[shape_of((mat.shape[2], width), F32)] * 2,
        in_specs=[VM] * (n + 1),
        out_specs=[VM] * 2,
        scratch_shapes=[pltpu.VMEM((n * size // 2, width), BF)],
        compiler_params=PARAMS,
    )(mat, *pieces)


def join_kernel(a_ref, b_ref, o_ref):
    o_ref[...] = (a_ref[...] + b_ref[...]).astype(BF)


def join(a, b):
    return pl.pallas_call(
        join_kernel,
        out_shape=shape_of(a.shape, BF),
        in_specs=[VM] * 2,
        out_specs=VM,
        compiler_params=PARAMS,
        name="join",
    )(a, b)


def fold_kernel(nx, ny, *refs):
    a, b = refs[:nx], refs[nx : nx + ny]
    outs = refs[nx + ny :]
    for k in range(ny):
        total = a[0][k].astype(F32)
        for r in a[1:]:
            total = total + r[k].astype(F32)
        outs[k][...] = total.astype(outs[k].dtype)
    for k in range(nx):
        total = b[0][k].astype(F32)
        for r in b[1:]:
            total = total + r[k].astype(F32)
        outs[ny + k][...] = total.astype(outs[ny + k].dtype)


def fold(a, b):
    nx, ny = len(a), len(b)
    _, block, half = a[0].shape
    mine, theirs = shape_of((block, half), F32), shape_of((block, half), BF)
    out = pl.pallas_call(
        functools.partial(fold_kernel, nx, ny),
        out_shape=[mine] + [theirs] * (ny - 1) + [mine] + [theirs] * (nx - 1),
        in_specs=[VM] * (nx + ny),
        out_specs=[VM] * (nx + ny),
        compiler_params=PARAMS,
        name="fold",
    )(*a, *b)
    return out[:ny], out[ny:]


def last_kernel(na, nb, *refs):
    a, b = refs[:na], refs[na : na + nb]
    gate, up, down = refs[na + nb :]
    left, right = a[0][...], b[0][...]
    for r in a[1:]:
        left = left + r[...].astype(F32)
    for r in b[1:]:
        right = right + r[...].astype(F32)
    fw = gate.shape[2]
    cut = left.shape[1] - fw
    gate[:, 0, :] = left[:, :fw]
    up[:, 0, :cut] = left[:, fw:]
    up[:, 0, cut:] = right[:, : fw - cut]
    down[:, 0, :] = right[:, fw - cut :]


def last(a, b):
    block, half = a[0].shape
    fw = 2 * half // 3
    return pl.pallas_call(
        functools.partial(last_kernel, len(a), len(b)),
        out_shape=[shape_of((block, 1, fw), F32)] * 3,
        in_specs=[VM] * (len(a) + len(b)),
        out_specs=[VM] * 3,
        compiler_params=PARAMS,
        name="last",
    )(*a, *b)


def per_device(tokens, cotangent, expert_ids, gate_values, w_gate, w_up, w_down):
    owners = lax.axis_size("expert")
    groups = lax.axis_size("dp")
    nx = int(round(groups**0.5))
    ny = groups // nx
    cap = tokens.shape[0] // 4
    width, _, fw = w_gate.shape
    wg, wu, wd = (w.reshape(width, fw) for w in (w_gate, w_up, w_down))
    moves = [0] + far_first(owners // 2)
    me = lax.axis_index("expert").astype(jnp.int32)[None]
    group = lax.axis_index("dp").astype(jnp.int32)
    xy = jnp.stack([group // ny, lax.rem(group, ny)])

    def send(pieces, sign):
        return [pieces[0]] + [
            lax.ppermute(p, "expert", pairs_of(owners, sign * m, 0))
            for p, m in zip(pieces[1:], moves[1:])
        ]

    def swap(piece):
        return lax.ppermute(piece, "expert", pairs_of(owners, 0, 1))

    def shift(piece, dx, dy):
        pairs = [
            (x * ny + y, ((x + dx) % nx) * ny + (y + dy) % ny) for x in range(nx) for y in range(ny)
        ]
        return lax.ppermute(piece, "dp", pairs)

    ids, gates = expert_ids.T, gate_values.T
    ids = (ids, swap(ids))
    tokens = (tokens, swap(tokens))
    *x_out, sel = make_slots(me, ids, tokens, moves, owners, cap)
    x_in = send(x_out, 1)
    gates = (gates, swap(gates))
    cots = (cotangent, swap(cotangent))
    *z_out, wt = make_gated(me, ids, gates, cots, sel, moves, owners, cap)
    z_in = send(z_out, 1)
    rows, gp, up, hid, *s_out = forward(x_in, wg, wu, wd)
    s_in = send(s_out, -1)
    fg, fu = factors(gp, up)
    zrows, dg, du = backward(z_in, wd, fg, fu)
    parts = wgrads(xy, rows, zrows, dg, du, hid, nx, ny)
    a, b = parts[:nx], parts[nx:]
    a_in, b_in = [a[0]], [b[0]]
    for d in far_first(nx):
        a_in.append(shift(a[d], d, 0))
    for d in far_first(ny):
        b_in.append(shift(b[d], 0, d))
    d_out = slot_dx(dg, du, wg, wu, len(moves))
    d_in = send(d_out, -1)
    s_mine, s_theirs = combine(wt, s_in, 3)
    s_got = swap(s_theirs)
    output = join(s_mine, s_got)
    a2, b2 = fold(a_in, b_in)
    a3, b3 = [a2[0]], [b2[0]]
    for d in far_first(ny):
        a3.append(shift(a2[d], 0, d))
    for d in far_first(nx):
        b3.append(shift(b2[d], d, 0))
    d_mine, d_theirs = combine(sel, d_in, 1)
    d_got = swap(d_theirs)
    grad_input = join(d_mine, d_got)
    grads = last(a3, b3)
    return (output, grad_input, *grads)


def solution(mesh):
    return jax.shard_map(
        per_device,
        mesh=mesh,
        in_specs=(
            P(("dp", "expert"), None),
            P(("dp", "expert"), None),
            P(("dp", "expert"), None),
            P(("dp", "expert"), None),
            P(None, "expert", None),
            P(None, "expert", None),
            P(None, "expert", None),
        ),
        out_specs=(
            P(("dp", "expert"), None),
            P(("dp", "expert"), None),
            P("dp", "expert", None),
            P("dp", "expert", None),
            P("dp", "expert", None),
        ),
        check_vma=False,
    )
```

```python
import functools

import jax
import jax.numpy as jnp
from jax import lax
from jax.experimental import pallas as pl
from jax.experimental.pallas import tpu as pltpu
from jax.sharding import PartitionSpec as P


STACK_IN = False
STACK_S = True
STACK_D = False
BF = jnp.bfloat16
F32 = jnp.float32
ANY = pl.BlockSpec(memory_space=pl.ANY)
HBM = pl.BlockSpec(memory_space=pltpu.HBM)
VM = pl.BlockSpec(memory_space=pltpu.VMEM)
SM = pl.BlockSpec(memory_space=pltpu.SMEM)
PARAMS = pltpu.CompilerParams(vmem_limit_bytes=24 * 1024 * 1024)


def shape_of(shape, dtype):
    return jax.ShapeDtypeStruct(shape, dtype)


def far_first(n):
    return sorted(range(1, n), key=lambda d: -min(d, n - d))


def pairs_of(owners, chip, core):
    chips = owners // 2
    return [
        (z * 2 + c, ((z + chip) % chips) * 2 + (c ^ core)) for z in range(chips) for c in range(2)
    ]


def target(me, chip, chips):
    return lax.rem(me // 2 + chip, chips) * 2 + lax.rem(me, 2)


def place(outs, me, moves, sign, j, rows, cols=slice(None)):
    if len(outs) > 1:
        outs[j][rows[0] : rows[1], cols] = rows[2]
    else:
        chips = outs[0].shape[0]
        at = lax.rem(me // 2 + sign * moves[j] + chips, chips)
        outs[0][at, rows[0] : rows[1], cols] = rows[2]


def pick(pieces, me, moves, sign, j, lo, hi):
    if len(pieces) > 1:
        return pieces[j][lo:hi, :]
    chips = pieces[0].shape[0]
    return pieces[0][lax.rem(me // 2 + sign * moves[j] + chips, chips), lo:hi, :]


def piece_shapes(stacked, n, size, width, dtype):
    if stacked:
        return [shape_of((n, size, width), dtype)]
    return [shape_of((size, width), dtype)] * n


def slots_kernel(moves, owners, cap, me_ref, *refs):
    sources, outs = refs[:4], refs[4:-5]
    sel_ref, rank_s, ids_s, tok_s, sems = refs[-5:]
    targets = [ids_s.at[0], ids_s.at[1], tok_s.at[0], tok_s.at[1]]
    copies = [
        pltpu.make_async_copy(a, b, sems.at[i])
        for i, (a, b) in enumerate(zip(sources, targets))
    ]
    for c in copies:
        c.start()
    _, topk, toks = ids_s.shape
    expert = lax.broadcasted_iota(jnp.int32, (owners, toks), 0)
    slot = lax.broadcasted_iota(jnp.int32, (cap, toks), 0)
    before = lax.broadcasted_iota(jnp.int32, (toks, toks), 0) < lax.broadcasted_iota(
        jnp.int32, (toks, toks), 1
    )
    before = jnp.where(before, 1.0, 0.0).astype(BF)
    for p in range(2):
        copies[p].wait()
        present = jnp.zeros((owners, toks), F32)
        for k in range(topk):
            present = present + jnp.where(ids_s[p, k : k + 1, :] == expert, 1.0, 0.0)
        earlier = jnp.dot(present.astype(BF), before, preferred_element_type=F32)
        rank_s[p] = jnp.where(present > 0.0, earlier, -1.0).astype(jnp.int32)
    for p in range(2):
        for j, move in enumerate(moves):
            e = target(me_ref[0], move, owners // 2)
            hit = rank_s[p, pl.ds(e, 1), :] == slot
            sel_ref[p, j * cap : (j + 1) * cap, :] = jnp.where(hit, 1.0, 0.0).astype(BF)
        copies[2 + p].wait()
        rows = jnp.dot(sel_ref[p], tok_s[p], preferred_element_type=F32).astype(BF)
        for j in range(len(moves)):
            part = (p * cap, (p + 1) * cap, rows[j * cap : (j + 1) * cap, :])
            place(outs, me_ref[0], moves, 1, j, part)


def stay(a):
    return pltpu.with_memory_space_constraint(a, pltpu.HBM)


def make_slots(me, ids, tokens, moves, owners, cap, stacked):
    toks, width = tokens[0].shape
    n = len(moves)
    return pl.pallas_call(
        functools.partial(slots_kernel, moves, owners, cap),
        out_shape=piece_shapes(stacked, n, 2 * cap, width, BF) + [shape_of((2, n * cap, toks), BF)],
        in_specs=[SM] + [HBM, ANY] * 2,
        out_specs=[VM] * (2 if stacked else n + 1),
        scratch_shapes=[
            pltpu.VMEM((2, owners, toks), jnp.int32),
            pltpu.VMEM((2, *ids[0].shape), jnp.int32),
            pltpu.VMEM((2, toks, width), BF),
            pltpu.SemaphoreType.DMA((4,)),
        ],
        compiler_params=PARAMS,
        name="slots",
    )(me, stay(ids[0]), ids[1], stay(tokens[0]), tokens[1])


def gated_kernel(moves, owners, cap, me_ref, ids0, ids1, gates0, gates1, cot0, cot1, sel, *refs):
    outs = refs[:-2]
    wt_ref, gate_s = refs[-2:]
    topk, toks = ids0.shape
    expert = lax.broadcasted_iota(jnp.int32, (owners, toks), 0)
    for p, (ids, gates) in enumerate(((ids0, gates0), (ids1, gates1))):
        gate = jnp.zeros((owners, toks), F32)
        for k in range(topk):
            gate = gate + jnp.where(ids[k : k + 1, :] == expert, gates[k : k + 1, :], 0.0)
        gate_s[p] = gate
    for p, cot in enumerate((cot0, cot1)):
        for j, move in enumerate(moves):
            e = target(me_ref[0], move, owners // 2)
            part = pl.ds(j * cap, cap)
            wt_ref[p, part, :] = sel[p, part, :].astype(F32) * gate_s[p, pl.ds(e, 1), :]
        rows = jnp.dot(sel[p], cot[...], preferred_element_type=F32)
        rows = (rows * jnp.sum(wt_ref[p], axis=1, keepdims=True)).astype(BF)
        for j in range(len(moves)):
            part = (p * cap, (p + 1) * cap, rows[j * cap : (j + 1) * cap, :])
            place(outs, me_ref[0], moves, 1, j, part)


def make_gated(me, ids, gates, cots, sel, moves, owners, cap, stacked):
    toks, width = cots[0].shape
    n = len(moves)
    return pl.pallas_call(
        functools.partial(gated_kernel, moves, owners, cap),
        out_shape=piece_shapes(stacked, n, 2 * cap, width, BF) + [shape_of((2, n * cap, toks), F32)],
        in_specs=[SM] + [VM] * 7,
        out_specs=[VM] * (2 if stacked else n + 1),
        scratch_shapes=[pltpu.VMEM((2, owners, toks), F32)],
        compiler_params=PARAMS,
        name="gated",
    )(me, *ids, *gates, *cots, sel)


def gather_rows(pieces, me, moves, rows):
    size = pieces[0].shape[-2]
    for j in range(len(moves)):
        rows[j * size : (j + 1) * size, :] = pick(pieces, me, moves, -1, j, 0, size)
    return size


def forward_kernel(n, moves, me_ref, *refs):
    pieces = refs[:n]
    wg, wu, wd = refs[n : n + 3]
    rows, gp, up, hid = refs[n + 3 : n + 7]
    outs = refs[n + 7 :]
    size = gather_rows(pieces, me_ref[0], moves, rows)
    fw, width = wg.shape[1], wd.shape[0]
    step = min(256, fw)

    @pl.loop(0, fw // step)
    def _(i):
        part = pl.ds(pl.multiple_of(i * step, step), step)
        g = jnp.dot(rows[...], wg[:, part], preferred_element_type=F32)
        u = jnp.dot(rows[...], wu[:, part], preferred_element_type=F32)
        gp[:, part] = g
        up[:, part] = u
        hid[:, part] = (g * jax.nn.sigmoid(g) * u).astype(BF)

    wide = min(512, width)

    @pl.loop(0, width // wide)
    def _(i):
        part = pl.ds(pl.multiple_of(i * wide, wide), wide)
        out = lax.dot_general(
            hid[...], wd[part, :], (((1,), (1,)), ((), ())), preferred_element_type=F32
        ).astype(BF)
        for j in range(len(moves)):
            place(outs, me_ref[0], moves, -1, j, (0, size, out[j * size : (j + 1) * size, :]), part)


def forward(me, pieces, wg, wu, wd, moves, stacked):
    n = len(moves)
    size, width = pieces[0].shape[-2:]
    slots, fw = n * size, wg.shape[1]
    out_shape = [
        shape_of((slots, width), BF),
        shape_of((slots, fw), F32),
        shape_of((slots, fw), F32),
        shape_of((slots, fw), BF),
    ] + piece_shapes(stacked, n, size, width, BF)
    return pl.pallas_call(
        functools.partial(forward_kernel, len(pieces), moves),
        out_shape=out_shape,
        in_specs=[SM] + [VM] * (len(pieces) + 3),
        out_specs=[VM] * len(out_shape),
        compiler_params=PARAMS,
        name="forward",
    )(me, *pieces, wg, wu, wd)


def factors_kernel(gp, up, fg, fu):
    g = gp[...]
    s = jax.nn.sigmoid(g)
    fg[...] = up[...] * s * (1.0 + g * (1.0 - s))
    fu[...] = g * s


def factors(gp, up):
    slots, fw = gp.shape
    step = min(128, slots)
    some = pl.BlockSpec((step, fw), lambda i: (i, 0))
    return pl.pallas_call(
        factors_kernel,
        out_shape=[shape_of((slots, fw), F32)] * 2,
        grid=(slots // step,),
        in_specs=[some] * 2,
        out_specs=[some] * 2,
        compiler_params=PARAMS,
        name="factors",
    )(gp, up)


def backward_kernel(n, moves, me_ref, *refs):
    pieces = refs[:n]
    wd, fg, fu = refs[n : n + 3]
    rows, dg, du = refs[n + 3 :]
    gather_rows(pieces, me_ref[0], moves, rows)
    slots = rows.shape[0]
    step = min(256, slots)

    @pl.loop(0, slots // step)
    def _(i):
        part = pl.ds(pl.multiple_of(i * step, step), step)
        dh = jnp.dot(rows[part, :], wd[...], preferred_element_type=F32)
        dg[part, :] = (dh * fg[part, :]).astype(BF)
        du[part, :] = (dh * fu[part, :]).astype(BF)


def backward(me, pieces, wd, fg, fu, moves):
    n = len(pieces)
    slots, fw = fg.shape
    return pl.pallas_call(
        functools.partial(backward_kernel, n, moves),
        out_shape=[shape_of((slots, wd.shape[0]), BF), shape_of((slots, fw), BF), shape_of((slots, fw), BF)],
        in_specs=[SM] + [VM] * (n + 3),
        out_specs=[VM] * 3,
        compiler_params=PARAMS,
        name="backward",
    )(me, *pieces, wd, fg, fu)


def wgrad_kernel(nx, ny, xy_ref, x_ref, z_ref, dg_ref, du_ref, hid_ref, *refs):
    a_refs, b_refs = refs[:nx], refs[nx : nx + ny]
    acc, sems = refs[nx + ny :]
    jx = pl.program_id(0)
    fw = dg_ref.shape[1]
    half = 3 * fw // 2
    block = acc.shape[1] // ny
    dims = (((0,), (0,)), ((), ()))
    xb = x_ref[...]
    acc[jx, :, 0:fw] = lax.dot_general(xb, dg_ref[...], dims, preferred_element_type=F32).astype(BF)
    acc[jx, :, fw : 2 * fw] = lax.dot_general(
        xb, du_ref[...], dims, preferred_element_type=F32
    ).astype(BF)
    acc[jx, :, 2 * fw : 3 * fw] = lax.dot_general(
        z_ref[...], hid_ref[...], dims, preferred_element_type=F32
    ).astype(BF)

    def copies(j):
        out = []
        for k in range(ny):
            at = pl.ds(pl.multiple_of(lax.rem(xy_ref[1] + k, ny) * block, block), block)
            out.append((acc.at[j, at, pl.ds(0, half)], a_refs[j].at[k], sems.at[j, k, 0]))
            out.append((acc.at[j, at, pl.ds(half, half)], b_refs[k].at[j], sems.at[j, k, 1]))
        return out

    for j in range(nx):

        @pl.when(jx == j)
        def _(j=j):
            for c in copies(j):
                pltpu.make_async_copy(*c).start()

    @pl.when(jx == nx - 1)
    def _():
        for j in range(nx):
            for c in copies(j):
                pltpu.make_async_copy(*c).wait()


def wgrads(xy, rows, zrows, dg, du, hid, nx, ny):
    slots, width = rows.shape
    fw = dg.shape[1]
    wide = width // nx
    block = wide // ny
    half = 3 * fw // 2
    whole = pl.BlockSpec((slots, fw), lambda i, xy: (0, 0))
    cols = pl.BlockSpec((slots, wide), lambda i, xy: (0, lax.rem(xy[0] + i, nx)))
    return pl.pallas_call(
        functools.partial(wgrad_kernel, nx, ny),
        out_shape=[shape_of((ny, block, half), BF)] * nx + [shape_of((nx, block, half), BF)] * ny,
        grid_spec=pltpu.PrefetchScalarGridSpec(
            num_scalar_prefetch=1,
            grid=(nx,),
            in_specs=[cols, cols, whole, whole, whole],
            out_specs=[ANY] * (nx + ny),
            scratch_shapes=[
                pltpu.VMEM((nx, wide, 3 * fw), BF),
                pltpu.SemaphoreType.DMA((nx, ny, 2)),
            ],
        ),
        compiler_params=pltpu.CompilerParams(
            dimension_semantics=("arbitrary",), vmem_limit_bytes=24 * 1024 * 1024
        ),
        name="wgrads",
    )(xy, rows, zrows, dg, du, hid)


def slot_dx_kernel(moves, me_ref, dg_ref, du_ref, wg_ref, wu_ref, *outs):
    dims = (((1,), (1,)), ((), ()))
    size = outs[0].shape[-2]
    out = lax.dot_general(dg_ref[...], wg_ref[...], dims, preferred_element_type=F32)
    out = out + lax.dot_general(du_ref[...], wu_ref[...], dims, preferred_element_type=F32)
    out = out.astype(BF)
    for j in range(len(moves)):
        part = (0, size, out[j * size : (j + 1) * size, :])
        place(outs, me_ref[0], moves, -1, j, part)


def slot_dx(me, dg, du, wg, wu, moves, stacked):
    slots, fw = dg.shape
    width = wg.shape[0]
    n = len(moves)
    size = slots // n
    wide = min(512, width)
    whole = pl.BlockSpec((slots, fw), lambda i: (0, 0))
    some = pl.BlockSpec((wide, fw), lambda i: (i, 0))
    if stacked:
        outs = [pl.BlockSpec((n, size, wide), lambda i: (0, 0, i))]
    else:
        outs = [pl.BlockSpec((size, wide), lambda i: (0, i))] * n
    return pl.pallas_call(
        functools.partial(slot_dx_kernel, moves),
        out_shape=piece_shapes(stacked, n, size, width, BF),
        grid=(width // wide,),
        in_specs=[SM, whole, whole, some, some],
        out_specs=outs,
        compiler_params=PARAMS,
        name="slot_dx",
    )(me, dg, du, wg, wu)


def combine_kernel(n, moves, terms, me_ref, mat_ref, *refs):
    pieces = refs[:n]
    outs, rows = refs[n : n + 2], refs[n + 2]
    size = pieces[0].shape[-2]
    cap = size // 2
    dims = (((0,), (0,)), ((), ()))
    for p in (1, 0):
        for j in range(len(moves)):
            piece = pick(pieces, me_ref[0], moves, 1, j, p * cap, (p + 1) * cap)
            rows[j * cap : (j + 1) * cap, :] = piece
        left = mat_ref[p]
        highs = []
        for _ in range(terms):
            highs.append(left.astype(BF))
            left = left - highs[-1].astype(left.dtype)
        high = jnp.concatenate(highs, axis=1) if terms > 1 else highs[0]
        width = rows.shape[1]
        wide = min(512, width)

        @pl.loop(0, width // wide)
        def _(i, p=p, high=high):
            part = pl.ds(pl.multiple_of(i * wide, wide), wide)
            dot = lax.dot_general(high, rows[:, part], dims, preferred_element_type=F32)
            toks = outs[p].shape[0]
            total = dot[:toks, :]
            for k in range(1, terms):
                total = total + dot[k * toks : (k + 1) * toks, :]
            outs[p][:, part] = total


def combine(me, mat, pieces, terms, moves):
    n = len(pieces)
    size, width = pieces[0].shape[-2:]
    return pl.pallas_call(
        functools.partial(combine_kernel, n, moves, terms),
        out_shape=[shape_of((mat.shape[2], width), F32)] * 2,
        in_specs=[SM] + [VM] * (n + 1),
        out_specs=[VM] * 2,
        scratch_shapes=[pltpu.VMEM((len(moves) * size // 2, width), BF)],
        compiler_params=PARAMS,
    )(me, mat, *pieces)


def join_kernel(a_ref, b_ref, o_ref):
    o_ref[...] = (a_ref[...] + b_ref[...]).astype(BF)


def join(a, b):
    return pl.pallas_call(
        join_kernel,
        out_shape=shape_of(a.shape, BF),
        in_specs=[VM] * 2,
        out_specs=VM,
        compiler_params=PARAMS,
        name="join",
    )(a, b)


def fold_kernel(nx, ny, *refs):
    a, b = refs[:nx], refs[nx : nx + ny]
    outs = refs[nx + ny :]
    block = a[0].shape[1]
    step = min(32, block)

    @pl.loop(0, block // step)
    def _(i):
        part = pl.ds(pl.multiple_of(i * step, step), step)
        for k in range(ny):
            total = a[0][k, part, :].astype(F32)
            for r in a[1:]:
                total = total + r[k, part, :].astype(F32)
            outs[k][part, :] = total.astype(outs[k].dtype)
        for k in range(nx):
            total = b[0][k, part, :].astype(F32)
            for r in b[1:]:
                total = total + r[k, part, :].astype(F32)
            outs[ny + k][part, :] = total.astype(outs[ny + k].dtype)


def fold(a, b):
    nx, ny = len(a), len(b)
    _, block, half = a[0].shape
    mine, theirs = shape_of((block, half), F32), shape_of((block, half), BF)
    out = pl.pallas_call(
        functools.partial(fold_kernel, nx, ny),
        out_shape=[mine] + [theirs] * (ny - 1) + [mine] + [theirs] * (nx - 1),
        in_specs=[VM] * (nx + ny),
        out_specs=[VM] * (nx + ny),
        compiler_params=PARAMS,
        name="fold",
    )(*a, *b)
    return out[:ny], out[ny:]


def last_kernel(na, nb, *refs):
    a, b = refs[:na], refs[na : na + nb]
    gate, up, down = refs[na + nb :]
    left, right = a[0][...], b[0][...]
    for r in a[1:]:
        left = left + r[...].astype(F32)
    for r in b[1:]:
        right = right + r[...].astype(F32)
    fw = gate.shape[2]
    cut = left.shape[1] - fw
    gate[:, 0, :] = left[:, :fw]
    up[:, 0, :cut] = left[:, fw:]
    up[:, 0, cut:] = right[:, : fw - cut]
    down[:, 0, :] = right[:, fw - cut :]


def last(a, b):
    block, half = a[0].shape
    fw = 2 * half // 3
    return pl.pallas_call(
        functools.partial(last_kernel, len(a), len(b)),
        out_shape=[shape_of((block, 1, fw), F32)] * 3,
        in_specs=[VM] * (len(a) + len(b)),
        out_specs=[VM] * 3,
        compiler_params=PARAMS,
        name="last",
    )(*a, *b)


def per_device(tokens, cotangent, expert_ids, gate_values, w_gate, w_up, w_down):
    owners = lax.axis_size("expert")
    groups = lax.axis_size("dp")
    nx = int(round(groups**0.5))
    ny = groups // nx
    cap = tokens.shape[0] // 4
    width, _, fw = w_gate.shape
    wg, wu, wd = (w.reshape(width, fw) for w in (w_gate, w_up, w_down))
    moves = [0] + far_first(owners // 2)
    me = lax.axis_index("expert").astype(jnp.int32)[None]
    group = lax.axis_index("dp").astype(jnp.int32)
    xy = jnp.stack([group // ny, lax.rem(group, ny)])

    same_core = [[2 * z + c for z in range(owners // 2)] for c in range(2)]

    def send(pieces, sign):
        if len(pieces) == 1:
            return [
                lax.all_to_all(
                    pieces[0], "expert", 0, 0, tiled=True, axis_index_groups=same_core
                )
            ]
        return [pieces[0]] + [
            lax.ppermute(p, "expert", pairs_of(owners, sign * m, 0))
            for p, m in zip(pieces[1:], moves[1:])
        ]

    def swap(piece):
        return lax.ppermute(piece, "expert", pairs_of(owners, 0, 1))

    def shift(piece, dx, dy):
        pairs = [
            (x * ny + y, ((x + dx) % nx) * ny + (y + dy) % ny) for x in range(nx) for y in range(ny)
        ]
        return lax.ppermute(piece, "dp", pairs)

    ids, gates = expert_ids.T, gate_values.T
    ids = (ids, swap(ids))
    tokens = (tokens, swap(tokens))
    *x_out, sel = make_slots(me, ids, tokens, moves, owners, cap, STACK_IN)
    x_in = send(x_out, 1)
    gates = (gates, swap(gates))
    cots = (cotangent, swap(cotangent))
    *z_out, wt = make_gated(me, ids, gates, cots, sel, moves, owners, cap, STACK_IN)
    z_in = send(z_out, 1)
    rows, gp, up, hid, *s_out = forward(me, x_in, wg, wu, wd, moves, STACK_S)
    s_in = send(s_out, -1)
    fg, fu = factors(gp, up)
    zrows, dg, du = backward(me, z_in, wd, fg, fu, moves)
    parts = wgrads(xy, rows, zrows, dg, du, hid, nx, ny)
    a, b = parts[:nx], parts[nx:]
    a_in, b_in = [a[0]], [b[0]]
    for i in range(max(nx, ny) - 1):
        if i < nx - 1:
            a_in.append(shift(a[far_first(nx)[i]], far_first(nx)[i], 0))
        if i < ny - 1:
            b_in.append(shift(b[far_first(ny)[i]], 0, far_first(ny)[i]))
    d_out = slot_dx(me, dg, du, wg, wu, moves, STACK_D)
    d_in = send(d_out, -1)
    s_mine, s_theirs = combine(me, wt, s_in, 3, moves)
    s_got = swap(s_theirs)
    output = join(s_mine, s_got)
    a2, b2 = fold(a_in, b_in)
    a3, b3 = [a2[0]], [b2[0]]
    for i in range(max(nx, ny) - 1):
        if i < ny - 1:
            a3.append(shift(a2[far_first(ny)[i]], 0, far_first(ny)[i]))
        if i < nx - 1:
            b3.append(shift(b2[far_first(nx)[i]], far_first(nx)[i], 0))
    d_mine, d_theirs = combine(me, sel, d_in, 1, moves)
    d_got = swap(d_theirs)
    grad_input = join(d_mine, d_got)
    grads = last(a3, b3)
    return (output, grad_input, *grads)


def solution(mesh):
    return jax.shard_map(
        per_device,
        mesh=mesh,
        in_specs=(
            P(("dp", "expert"), None),
            P(("dp", "expert"), None),
            P(("dp", "expert"), None),
            P(("dp", "expert"), None),
            P(None, "expert", None),
            P(None, "expert", None),
            P(None, "expert", None),
        ),
        out_specs=(
            P(("dp", "expert"), None),
            P(("dp", "expert"), None),
            P("dp", "expert", None),
            P("dp", "expert", None),
            P("dp", "expert", None),
        ),
        check_vma=False,
    )
```
